32 devices in a mesh: seq: 16 (over z, y, x), head: 2 (over core).
Axes of the slice: x: 2, y: 2, z: 4, core: 2. Of those that a mesh axis runs over, the one named last changes fastest.
Arguments:
- block_in: bfloat16 [3072, 1024], P('seq'), may hold values from -6 to 6
- first_norm_gain: float32 [1024], replicated, may hold values from 0.25 to 1.75
- w_query: bfloat16 [1024, 1024], P('seq', 'head'), may hold values from -0.1875 to 0.1875
- w_key: bfloat16 [1024, 1024], P('seq', 'head'), may hold values from -0.1875 to 0.1875
- w_value: bfloat16 [1024, 2048], P('seq', 'head'), may hold values from -0.1875 to 0.1875
- w_gate: bfloat16 [1024, 2048], P('seq', 'head'), may hold values from -0.1875 to 0.1875
- w_alpha: bfloat16 [1024, 8], P('seq', 'head'), may hold values from -0.1875 to 0.1875
- w_beta: bfloat16 [1024, 8], P('seq', 'head'), may hold values from -0.1875 to 0.1875
- conv_query: float32 [4, 1024], P(None, 'head'), may hold values from -3 to 3
- conv_key: float32 [4, 1024], P(None, 'head'), may hold values from -3 to 3
- conv_value: float32 [4, 2048], P(None, 'head'), may hold values from -3 to 3
- a_log: float32 [8], P('head'), may hold values from -9 to 1
- dt_bias: float32 [8], P('head'), may hold values from -4 to 1
- out_gain: float32 [256], replicated, may hold values from 0.25 to 1.75
- w_out: bfloat16 [2048, 1024], P('head', 'seq'), may hold values from -0.1875 to 0.1875
- second_norm_gain: float32 [1024], replicated, may hold values from 0.25 to 1.75
- w_ffgate: bfloat16 [1024, 2816], P('seq', 'head'), may hold values from -0.1875 to 0.1875
- w_ffup: bfloat16 [1024, 2816], P('seq', 'head'), may hold values from -0.1875 to 0.1875
- w_ffdown: bfloat16 [2816, 1024], P('head', 'seq'), may hold values from -0.21875 to 0.21875
- cotangent: bfloat16 [3072, 1024], P('seq'), may hold values from -6 to 6
Outputs:
- block_out: bfloat16 [3072, 1024], P('seq')
- input_gradient: float32 [3072, 1024], P('seq')
- first_norm_gain_gradient: float32 [1024], replicated
- grad_query: float32 [1024, 1024], P('seq', 'head')
- grad_key: float32 [1024, 1024], P('seq', 'head')
- grad_value: float32 [1024, 2048], P('seq', 'head')
- grad_gate: float32 [1024, 2048], P('seq', 'head')
- grad_alpha: float32 [1024, 8], P('seq', 'head')
- grad_beta: float32 [1024, 8], P('seq', 'head')
- grad_convq: float32 [4, 1024], P(None, 'head')
- grad_convk: float32 [4, 1024], P(None, 'head')
- grad_convv: float32 [4, 2048], P(None, 'head')
- grad_alog: float32 [8], P('head')
- grad_dt: float32 [8], P('head')
- grad_outgain: float32 [256], replicated
- grad_out: float32 [2048, 1024], P('head', 'seq')
- second_norm_gain_gradient: float32 [1024], replicated
- grad_ffgate: float32 [1024, 2816], P('seq', 'head')
- grad_ffup: float32 [1024, 2816], P('seq', 'head')
- grad_ffdown: float32 [2816, 1024], P('head', 'seq')
The draws below stay inside these ranges and needn't reach their ends.
All inputs are finite; a program needn't handle non-finite values.
Results may differ from the reference program's by a relative error of at most 0.02.
The reference program's roundings to bfloat16 on the way count: a program that leaves them out, or rounds other values in their place, can miss the bound.
Values may be sent and summed in bfloat16 or wider, within the bound.
A program may use at most 384 MiB of HBM per device.

```python
import jax
import jax.numpy as jnp
from jax import lax

D = 1024
H = 8
DK = 128
DV = 256
FF = 2816
CONV = 4
SPAN = 64
LENGTH = 3072


def level_of(rng, shape, cuts, low, largest):
    def one(dim, blocks):
        heights = jax.random.uniform(jax.random.fold_in(jax.random.fold_in(rng, 6), dim), (blocks,), jnp.float32, low / len(cuts), largest / len(cuts))
        return jnp.repeat(jnp.exp(heights), shape[dim] // blocks).reshape((-1,) + (1,) * (len(shape) - dim - 1))

    factor_of = one(*cuts[0])
    for cut in cuts[1:]:
        factor_of = factor_of * one(*cut)
    return factor_of


def centred(own_key, dims, spread, most, cuts=(), kind=jnp.bfloat16):
    result = jax.random.normal(own_key, dims, jnp.float32) * spread
    if len(cuts) > 0:
        result = level_of(own_key, dims, cuts, -0.22, 0.18) * result
    return jnp.clip(result, min=-most, max=most).astype(kind)


def setup_inputs(seed: int = 0) -> dict:
    arg_keys = jax.random.split(jax.random.key(seed), 21)
    return {
        "block_in": centred(arg_keys[0], (LENGTH, D), 1.0, 6.0, ((0, 16),)),
        "first_norm_gain": jnp.clip(1.0 + 0.15 * jax.random.normal(arg_keys[1], (D,), jnp.float32), 0.25, 1.75),
        "w_query": centred(arg_keys[2], (D, H * DK), D ** -0.5, 0.1875, ((0, 16), (1, 2))),
        "w_key": centred(arg_keys[3], (D, H * DK), D ** -0.5, 0.1875, ((0, 16), (1, 2))),
        "w_value": centred(arg_keys[4], (D, H * DV), D ** -0.5, 0.1875, ((0, 16), (1, 2))),
        "w_gate": centred(arg_keys[5], (D, H * DV), D ** -0.5, 0.1875, ((0, 16), (1, 2))),
        "w_alpha": centred(arg_keys[6], (D, H), D ** -0.5, 0.1875, ((0, 16), (1, 2))),
        "w_beta": centred(arg_keys[7], (D, H), D ** -0.5, 0.1875, ((0, 16), (1, 2))),
        "conv_query": centred(arg_keys[8], (CONV, H * DK), 0.5, 3.0, ((1, 2),), jnp.float32),
        "conv_key": centred(arg_keys[9], (CONV, H * DK), 0.5, 3.0, ((1, 2),), jnp.float32),
        "conv_value": centred(arg_keys[10], (CONV, H * DV), 0.5, 3.0, ((1, 2),), jnp.float32),
        "a_log": jnp.clip(-9.0 + 10.0 * jax.random.uniform(arg_keys[11], (H,), jnp.float32) ** level_of(arg_keys[11], (H,), ((0, 2),), -0.2, 0.2), -9.0, 1.0),
        "dt_bias": jnp.clip(-4.0 + 5.0 * jax.random.uniform(arg_keys[12], (H,), jnp.float32) ** level_of(arg_keys[12], (H,), ((0, 2),), -0.2, 0.2), -4.0, 1.0),
        "out_gain": jnp.clip(1.0 + 0.15 * jax.random.normal(arg_keys[13], (DV,), jnp.float32), 0.25, 1.75),
        "w_out": centred(arg_keys[14], (H * DV, D), (H * DV // 2) ** -0.5, 0.1875, ((0, 2), (1, 16))),
        "second_norm_gain": jnp.clip(1.0 + 0.15 * jax.random.normal(arg_keys[15], (D,), jnp.float32), 0.25, 1.75),
        "w_ffgate": centred(arg_keys[16], (D, FF), D ** -0.5, 0.1875, ((0, 16), (1, 2))),
        "w_ffup": centred(arg_keys[17], (D, FF), D ** -0.5, 0.1875, ((0, 16), (1, 2))),
        "w_ffdown": centred(arg_keys[18], (FF, D), (FF // 4) ** -0.5, 0.21875, ((0, 2), (1, 16))),
        "cotangent": centred(arg_keys[19], (LENGTH, D), 1.0, 6.0, ((0, 16),)),
    }


MATMUL_ACCURACY = lax.Precision.HIGHEST
EPS_NORM = 1e-06
EPS_HEAD = 1e-05
EPS_UNIT = 1e-06

def matmul(left, right):
    return jnp.dot(left.astype(jnp.float32), right.astype(jnp.float32), preferred_element_type=jnp.float32)

def matmul_tl(left, right):
    return lax.dot_general(left.astype(jnp.float32), right.astype(jnp.float32), (((0,), (0,)), ((), ())), preferred_element_type=jnp.float32)

def matmul_tr(left, right):
    return lax.dot_general(left.astype(jnp.float32), right.astype(jnp.float32), (((1,), (1,)), ((), ())), preferred_element_type=jnp.float32)

def rms_scale(values):
    return lax.rsqrt(lax.optimization_barrier(jnp.mean(values * values, axis=-1, keepdims=True)) + EPS_NORM)

def norm_gradient_step(unit_input_gradient, unit_input, inverse_scale):
    return inverse_scale * (unit_input_gradient - unit_input * lax.optimization_barrier(jnp.mean(unit_input_gradient * unit_input, axis=-1, keepdims=True)))

def conv_apply(extended, weight, rows):
    total = weight[0] * extended[0:rows]
    for tap in range(1, CONV):
        total = total + weight[tap] * extended[tap:tap + rows]
    return total

def conv_back_apply(extended, weight, rows):
    total = weight[0] * extended[CONV - 1:CONV - 1 + rows]
    for tap in range(1, CONV):
        total = total + weight[tap] * extended[CONV - 1 - tap:CONV - 1 - tap + rows]
    return total

def conv_weight_grad(grad_out, extended, rows):
    return jnp.stack([lax.optimization_barrier(jnp.sum(grad_out * extended[tap:tap + rows], axis=0)) for tap in range(CONV)], axis=0)

def prepare(qc, kc, vc, b_lin, a_lin, a_log, dt_bias):
    heads = a_log.shape[0]
    rows = qc.shape[0]
    q_act = jax.nn.silu(qc).reshape(rows, heads, -1)
    k_act = jax.nn.silu(kc).reshape(rows, heads, -1)
    dim_k = q_act.shape[-1]
    query = q_act * lax.rsqrt(lax.optimization_barrier(jnp.sum(q_act * q_act, axis=-1, keepdims=True)) + EPS_UNIT) * dim_k ** (-0.5)
    keyvec = k_act * lax.rsqrt(lax.optimization_barrier(jnp.sum(k_act * k_act, axis=-1, keepdims=True)) + EPS_UNIT)
    value = jax.nn.silu(vc).reshape(rows, heads, -1)
    beta = jax.nn.sigmoid(b_lin).T
    logdec = (-jnp.exp(a_log)[None, :] * jax.nn.softplus(a_lin + dt_bias[None, :])).T
    return (jnp.transpose(query, (1, 0, 2)), jnp.transpose(keyvec, (1, 0, 2)), jnp.transpose(value, (1, 0, 2)), beta, logdec)

def span_terms(query, keyvec, value, beta, logdec):
    size = query.shape[1]
    dim_k = keyvec.shape[-1]
    dim_v = value.shape[-1]
    cumul = jnp.cumsum(logdec, axis=-1)
    index = jnp.arange(size)
    strict = index[:, None] > index[None, :]
    weak = index[:, None] >= index[None, :]
    diff = cumul[:, :, None] - cumul[:, None, :]
    decay = jnp.where(weak, jnp.exp(jnp.where(weak, diff, 0.0)), 0.0)
    kk = jnp.einsum('hck,hdk->hcd', keyvec, keyvec, precision=MATMUL_ACCURACY)
    lower = jnp.where(strict, beta[:, :, None] * decay * kk, 0.0) + jnp.eye(size, dtype=query.dtype)
    rhs = jnp.concatenate([beta[:, :, None] * value, (beta * jnp.exp(cumul))[:, :, None] * keyvec], axis=-1)
    solved = lax.linalg.triangular_solve(lower, rhs, left_side=True, lower=True, unit_diagonal=True)
    starting_value = solved[..., :dim_v]
    mixk = solved[..., dim_v:]
    scores = jnp.einsum('hck,hdk->hcd', query, keyvec, precision=MATMUL_ACCURACY) * decay
    empty_output = jnp.einsum('hcd,hdv->hcv', scores, starting_value, precision=MATMUL_ACCURACY)
    extent = jnp.exp(cumul)[:, :, None] * query - jnp.einsum('hcd,hdk->hck', scores, mixk, precision=MATMUL_ACCURACY)
    trailing_rows = jnp.exp(cumul[:, -1:] - cumul)[:, :, None] * keyvec
    state_matrix = jnp.exp(cumul[:, -1])[:, None, None] * jnp.eye(dim_k, dtype=query.dtype) - jnp.einsum('hck,hcj->hkj', trailing_rows, mixk, precision=MATMUL_ACCURACY)
    addend_update = jnp.einsum('udw,udf->uwf', trailing_rows, starting_value, precision=MATMUL_ACCURACY)
    return (empty_output, extent, state_matrix, addend_update)

def delta_all(query, keyvec, value, beta, logdec):
    heads, rows, dim_k = query.shape
    blocks = rows // SPAN

    def split(array):
        return jnp.moveaxis(array.reshape((heads, blocks, SPAN) + array.shape[2:]), 1, 0)

    @jax.checkpoint
    def step(memory_state, item):
        empty_output, extent, state_matrix, addend_update = span_terms(*item)
        block_result = empty_output + jnp.einsum('aow,awr->aor', extent, memory_state, precision=MATMUL_ACCURACY)
        memory_state = jnp.einsum('sug,sgc->suc', state_matrix, memory_state, precision=MATMUL_ACCURACY) + addend_update
        return (memory_state, block_result)
    init = jnp.zeros((heads, dim_k, value.shape[-1]), query.dtype)
    _, outputs = lax.scan(step, init, (split(query), split(keyvec), split(value), split(beta), split(logdec)))
    return jnp.moveaxis(outputs, 0, 1).reshape(heads, rows, -1)

def finish(block_result, gate_pre, out_gain):
    heads, rows, dim_v = block_result.shape
    normed = block_result * lax.rsqrt(lax.optimization_barrier(jnp.mean(block_result * block_result, axis=-1, keepdims=True)) + EPS_HEAD) * out_gain
    gating = jax.nn.silu(gate_pre).reshape(rows, heads, dim_v)
    return (jnp.transpose(normed, (1, 0, 2)) * gating).reshape(rows, heads * dim_v)

def mixer_core(qc, kc, vc, b_lin, a_lin, a_log, dt_bias, gate_pre, out_gain):
    return finish(delta_all(*prepare(qc, kc, vc, b_lin, a_lin, a_log, dt_bias)), gate_pre, out_gain)

def reference(block_in, first_norm_gain, w_query, w_key, w_value, w_gate, w_alpha, w_beta, conv_query, conv_key, conv_value, a_log, dt_bias, out_gain, w_out, second_norm_gain, w_ffgate, w_ffup, w_ffdown, cotangent):
    rows = block_in.shape[0]
    input_float = block_in.astype(jnp.float32)
    first_inverse_scale = rms_scale(input_float)
    first_unit_input = input_float * first_inverse_scale
    first_normed_input = (first_unit_input * first_norm_gain).astype(jnp.bfloat16)
    qpre = matmul(first_normed_input, w_query).astype(jnp.bfloat16)
    kpre = matmul(first_normed_input, w_key).astype(jnp.bfloat16)
    vpre = matmul(first_normed_input, w_value).astype(jnp.bfloat16)
    gpre = matmul(first_normed_input, w_gate).astype(jnp.bfloat16)
    a_lin = matmul(first_normed_input, w_alpha)
    b_lin = matmul(first_normed_input, w_beta)
    front = ((CONV - 1, 0), (0, 0))
    q_ext = jnp.pad(qpre.astype(jnp.float32), front)
    k_ext = jnp.pad(kpre.astype(jnp.float32), front)
    v_ext = jnp.pad(vpre.astype(jnp.float32), front)
    qc = conv_apply(q_ext, conv_query, rows)
    kc = conv_apply(k_ext, conv_key, rows)
    vc = conv_apply(v_ext, conv_value, rows)
    on_f, core_back = jax.vjp(mixer_core, qc, kc, vc, b_lin, a_lin, a_log, dt_bias, gpre.astype(jnp.float32), out_gain)
    on_b = on_f.astype(jnp.bfloat16)
    hidden_residual = input_float + matmul(on_b, w_out)
    second_inverse_scale = rms_scale(hidden_residual)
    second_unit_input = hidden_residual * second_inverse_scale
    second_normed_input = (second_unit_input * second_norm_gain).astype(jnp.bfloat16)
    fg = matmul(second_normed_input, w_ffgate)
    fu = matmul(second_normed_input, w_ffup)
    hid = (jax.nn.silu(fg) * fu).astype(jnp.bfloat16)
    block_out = (hidden_residual + matmul(hid, w_ffdown)).astype(jnp.bfloat16)
    feedforward_output_gradient = cotangent.astype(jnp.float32)
    grad_ffdown = matmul_tl(hid, cotangent)
    dhid = matmul_tr(cotangent, w_ffdown)
    sig = jax.nn.sigmoid(fg)
    dfu = (dhid * fg * sig).astype(jnp.bfloat16)
    dfg = (dhid * fu * sig * (1.0 + fg * (1.0 - sig))).astype(jnp.bfloat16)
    grad_ffgate = matmul_tl(second_normed_input, dfg)
    grad_ffup = matmul_tl(second_normed_input, dfu)
    second_normed_gradient = matmul_tr(dfg, w_ffgate) + matmul_tr(dfu, w_ffup)
    second_norm_gain_gradient = lax.optimization_barrier(jnp.sum(second_normed_gradient * second_unit_input, axis=0))
    hidden_gradient = feedforward_output_gradient + norm_gradient_step(second_normed_gradient * second_norm_gain, second_unit_input, second_inverse_scale)
    dh_b = hidden_gradient.astype(jnp.bfloat16)
    grad_out = matmul_tl(on_b, dh_b)
    don = matmul_tr(dh_b, w_out)
    dqc, dkc, dvc, db_lin, da_lin, grad_alog, grad_dt, dgpre, grad_outgain = core_back(don)
    back = ((0, CONV - 1), (0, 0))
    grad_convq = conv_weight_grad(dqc, q_ext, rows)
    grad_convk = conv_weight_grad(dkc, k_ext, rows)
    grad_convv = conv_weight_grad(dvc, v_ext, rows)
    dqb = conv_back_apply(jnp.pad(dqc, back), conv_query, rows).astype(jnp.bfloat16)
    dkb = conv_back_apply(jnp.pad(dkc, back), conv_key, rows).astype(jnp.bfloat16)
    dvb = conv_back_apply(jnp.pad(dvc, back), conv_value, rows).astype(jnp.bfloat16)
    dgb = dgpre.astype(jnp.bfloat16)
    dab = da_lin.astype(jnp.bfloat16)
    dbb = db_lin.astype(jnp.bfloat16)
    grad_query = matmul_tl(first_normed_input, dqb)
    grad_key = matmul_tl(first_normed_input, dkb)
    grad_value = matmul_tl(first_normed_input, dvb)
    grad_gate = matmul_tl(first_normed_input, dgb)
    grad_alpha = matmul_tl(first_normed_input, dab)
    grad_beta = matmul_tl(first_normed_input, dbb)
    first_normed_gradient = matmul_tr(dqb, w_query) + matmul_tr(dkb, w_key) + matmul_tr(dvb, w_value) + matmul_tr(dgb, w_gate) + matmul_tr(dab, w_alpha) + matmul_tr(dbb, w_beta)
    first_norm_gain_gradient = lax.optimization_barrier(jnp.sum(first_normed_gradient * first_unit_input, axis=0))
    input_gradient = hidden_gradient + norm_gradient_step(first_normed_gradient * first_norm_gain, first_unit_input, first_inverse_scale)
    return (block_out, input_gradient, first_norm_gain_gradient, grad_query, grad_key, grad_value, grad_gate, grad_alpha, grad_beta, grad_convq, grad_convk, grad_convv, grad_alog, grad_dt, grad_outgain, grad_out, second_norm_gain_gradient, grad_ffgate, grad_ffup, grad_ffdown)
```

```python
import functools

import jax
import jax.numpy as jnp
from jax import lax
from jax.experimental import pallas as pl
from jax.experimental.pallas import tpu as pltpu
from jax.sharding import PartitionSpec as P

CONV = 4
SPAN = 64


EPS_NORM = 1e-06
EPS_HEAD = 1e-05
EPS_UNIT = 1e-06


def from_behind(block, axis, distance):
    devices = range(lax.axis_size(axis))
    route = [(i - distance, i) for i in devices if i - distance in devices]
    return lax.ppermute(block, axis, route)


def pair_sum(block):
    return block + lax.ppermute(block, "head", [(0, 1), (1, 0)])


def matmul(left, right):
    return jnp.dot(left, right, preferred_element_type=jnp.float32)


def matmul_tl(left, right):
    return lax.dot_general(
        left, right, (((0,), (0,)), ((), ())), preferred_element_type=jnp.float32
    )


def matmul_tr(left, right):
    return lax.dot_general(
        left, right, (((1,), (1,)), ((), ())), preferred_element_type=jnp.float32
    )


def rms_scale(values):
    return lax.rsqrt(jnp.mean(values * values, axis=-1, keepdims=True) + EPS_NORM)


def norm_gradient_step(unit_input_gradient, unit_input, inverse_scale):
    return inverse_scale * (
        unit_input_gradient
        - unit_input * jnp.mean(unit_input_gradient * unit_input, axis=-1, keepdims=True)
    )


def conv_apply(extended, weight, rows):
    total = weight[0] * extended[0:rows]
    for tap in range(1, CONV):
        total = total + weight[tap] * extended[tap : tap + rows]
    return total


def conv_back_apply(extended, weight, rows):
    total = weight[0] * extended[CONV - 1 : CONV - 1 + rows]
    for tap in range(1, CONV):
        total = total + weight[tap] * extended[CONV - 1 - tap : CONV - 1 - tap + rows]
    return total


def conv_weight_grad(grad_out, extended, rows):
    return jnp.stack(
        [jnp.sum(grad_out * extended[tap : tap + rows], axis=0) for tap in range(CONV)], axis=0
    )


def prepare(qc, kc, vc, b_lin, a_lin, a_log, dt_bias):
    heads = a_log.shape[0]
    rows = qc.shape[0]
    q_act = jax.nn.silu(qc).reshape(rows, heads, -1)
    k_act = jax.nn.silu(kc).reshape(rows, heads, -1)
    dim_k = q_act.shape[-1]
    query = (
        q_act
        * lax.rsqrt(jnp.sum(q_act * q_act, axis=-1, keepdims=True) + EPS_UNIT)
        * dim_k ** (-0.5)
    )
    keyvec = k_act * lax.rsqrt(jnp.sum(k_act * k_act, axis=-1, keepdims=True) + EPS_UNIT)
    value = jax.nn.silu(vc).reshape(rows, heads, -1)
    beta = jax.nn.sigmoid(b_lin).T
    logdec = (-jnp.exp(a_log)[None, :] * jax.nn.softplus(a_lin + dt_bias[None, :])).T
    return (
        jnp.transpose(query, (1, 0, 2)),
        jnp.transpose(keyvec, (1, 0, 2)),
        jnp.transpose(value, (1, 0, 2)),
        beta,
        logdec,
    )


def finish(block_result, gate_pre, out_gain):
    heads, rows, dim_v = block_result.shape
    normed = (
        block_result
        * lax.rsqrt(jnp.mean(block_result * block_result, axis=-1, keepdims=True) + EPS_HEAD)
        * out_gain
    )
    gating = jax.nn.silu(gate_pre).reshape(rows, heads, dim_v)
    return (jnp.transpose(normed, (1, 0, 2)) * gating).reshape(rows, heads * dim_v)


def halves(x):
    high = x.astype(jnp.bfloat16)
    return high, (x - high.astype(jnp.float32)).astype(jnp.bfloat16)


def raw_dot(a, b, ca, cb):
    a_high, a_low = halves(a)
    b_high, b_low = halves(b)

    def one(x, y):
        return lax.dot_general(
            x, y, (((ca,), (cb,)), ((), ())), preferred_element_type=jnp.float32
        )

    return one(a_high, b_high) + (one(a_high, b_low) + one(a_low, b_high))


@functools.partial(jax.custom_vjp, nondiff_argnums=(2, 3))
def dot(a, b, ca, cb):
    return raw_dot(a, b, ca, cb)


def dot_fwd(a, b, ca, cb):
    return raw_dot(a, b, ca, cb), (a, b)


def dot_bwd(ca, cb, kept, g):
    a, b = kept
    da = raw_dot(g, b, 1, 1 - cb) if ca == 1 else raw_dot(b, g, 1 - cb, 1)
    db = raw_dot(a, g, 1 - ca, 0) if cb == 0 else raw_dot(g, a, 0, 1 - ca)
    return da, db


dot.defvjp(dot_fwd, dot_bwd)


def raw_inverse(lower):
    size = lower.shape[0]
    row = lax.broadcasted_iota(jnp.int32, (size, size), 0)
    col = lax.broadcasted_iota(jnp.int32, (size, size), 1)
    result = jnp.where(row == col, 1.0, 0.0)
    width = 1
    while width < size:
        inside = (row // (2 * width) == col // (2 * width)) & (row // width != col // width)
        band = jnp.where(inside, lower, 0.0)
        if width == 1:
            result = result - band
        else:
            result = result - raw_dot(result, raw_dot(band, result, 1, 0), 1, 0)
        width = 2 * width
    return result


@jax.custom_vjp
def inverse(lower):
    return raw_inverse(lower)


def inverse_fwd(lower):
    result = raw_inverse(lower)
    return result, result


def inverse_bwd(result, g):
    return (-raw_dot(raw_dot(result, g, 0, 0), result, 1, 1),)


inverse.defvjp(inverse_fwd, inverse_bwd)


def span_terms(query, keyvec, value, beta, log_col, log_row):
    size, dim_k = query.shape
    row = lax.broadcasted_iota(jnp.int32, (size, size), 0)
    col = lax.broadcasted_iota(jnp.int32, (size, size), 1)
    strict = row > col
    weak = row >= col
    cum_col = jnp.sum(jnp.where(weak, log_row, 0.0), axis=1, keepdims=True)
    cum_row = jnp.sum(jnp.where(row <= col, log_col, 0.0), axis=0, keepdims=True)
    total = jnp.sum(log_col, axis=0, keepdims=True)
    after = jnp.sum(jnp.where(row < col, log_row, 0.0), axis=1, keepdims=True)
    decay = jnp.where(weak, jnp.exp(jnp.where(weak, cum_col - cum_row, 0.0)), 0.0)
    kk = dot(keyvec, keyvec, 1, 1)
    solver = inverse(jnp.where(strict, beta * decay * kk, 0.0))
    reach = jnp.exp(cum_col)
    starting_value = dot(solver, beta * value, 1, 0)
    mixk = dot(solver, (beta * reach) * keyvec, 1, 0)
    scores = dot(query, keyvec, 1, 1) * decay
    empty_output = dot(scores, starting_value, 1, 0)
    extent = reach * query - dot(scores, mixk, 1, 0)
    trailing = jnp.exp(after) * keyvec
    k_row = lax.broadcasted_iota(jnp.int32, (dim_k, dim_k), 0)
    k_col = lax.broadcasted_iota(jnp.int32, (dim_k, dim_k), 1)
    state_matrix = jnp.where(k_row == k_col, jnp.exp(total), 0.0) - dot(trailing, mixk, 0, 0)
    addend = dot(trailing, starting_value, 0, 0)
    return empty_output, extent, state_matrix, addend


def spans_kernel(q, k, v, b, lc, lr, empty, extent, matrix, addend, product, running):
    heads, dim_k = q.shape[1], q.shape[3]

    @pl.when(pl.program_id(0) == 0)
    def _():
        k_row = lax.broadcasted_iota(jnp.int32, (dim_k, dim_k), 0)
        k_col = lax.broadcasted_iota(jnp.int32, (dim_k, dim_k), 1)
        for h in range(heads):
            product[h] = jnp.where(k_row == k_col, 1.0, 0.0)
            running[h] = jnp.zeros(running.shape[1:], jnp.float32)

    for h in range(heads):
        e, x, m, a = span_terms(q[0, h], k[0, h], v[0, h], b[0, h], lc[0, h], lr[0, h])
        empty[0, h] = e
        extent[0, h] = x
        matrix[0, h] = m
        addend[0, h] = a
        product[h] = raw_dot(m, product[h], 1, 0)
        running[h] = raw_dot(m, running[h], 1, 0) + a


def apply_kernel(empty, extent, matrix, addend, start, out, states, state):
    heads = empty.shape[1]

    @pl.when(pl.program_id(0) == 0)
    def _():
        state[...] = start[...]

    for h in range(heads):
        s = state[h]
        states[0, h] = s
        out[0, h] = empty[0, h] + raw_dot(extent[0, h], s, 1, 0)
        state[h] = raw_dot(matrix[0, h], s, 1, 0) + addend[0, h]


def partial_kernel(extent, matrix, grad, result):
    heads = extent.shape[1]

    @pl.when(pl.program_id(0) == 0)
    def _():
        result[...] = jnp.zeros(result.shape, jnp.float32)

    for h in range(heads):
        result[h] = raw_dot(matrix[0, h], result[h], 0, 0) + raw_dot(
            extent[0, h], grad[0, h], 0, 0
        )


def back_kernel(
    q, k, v, b, lc, lr, extent, matrix, states, grad, end, dq, dk, dv, db, dlc, dlr, later
):
    heads = q.shape[1]

    @pl.when(pl.program_id(0) == 0)
    def _():
        later[...] = end[...]

    for h in range(heads):
        g_state = later[h]
        g_out = grad[0, h]
        s = states[0, h]
        args = (q[0, h], k[0, h], v[0, h], b[0, h], lc[0, h], lr[0, h])
        _, back = jax.vjp(span_terms, *args)
        d = back((g_out, raw_dot(g_out, s, 1, 1), raw_dot(g_state, s, 1, 1), g_state))
        for ref, part in zip((dq, dk, dv, db, dlc, dlr), d):
            ref[0, h] = part
        later[h] = raw_dot(matrix[0, h], g_state, 0, 0) + raw_dot(extent[0, h], g_out, 0, 0)


def chain_kernel(reverse, matrices, addends, out):
    n = matrices.shape[0]

    def turn(i, state):
        at = n - 1 - i if reverse else i
        out[at] = state
        return raw_dot(matrices[at], state, 0 if reverse else 1, 0) + addends[at]

    lax.fori_loop(0, n, turn, jnp.zeros(out.shape[1:], jnp.float32))


def shape_of(array):
    return jax.ShapeDtypeStruct(array.shape, jnp.float32)


def over_blocks(kernel, blocks, whole_in, outs, whole_out, scratch, reverse, *arrays):
    def spec(shape, whole):
        rank = len(shape)
        if whole:
            return pl.BlockSpec(shape, lambda c: (0,) * rank)
        if reverse:
            return pl.BlockSpec((1,) + shape[1:], lambda c: (blocks - 1 - c,) + (0,) * (rank - 1))
        return pl.BlockSpec((1,) + shape[1:], lambda c: (c,) + (0,) * (rank - 1))

    cut = len(arrays) - whole_in
    return pl.pallas_call(
        kernel,
        grid=(blocks,),
        in_specs=[spec(a.shape, i >= cut) for i, a in enumerate(arrays)],
        out_specs=[spec(s, i >= len(outs) - whole_out) for i, s in enumerate(outs)],
        out_shape=[jax.ShapeDtypeStruct(s, jnp.float32) for s in outs],
        scratch_shapes=[pltpu.VMEM(s, jnp.float32) for s in scratch],
        compiler_params=pltpu.CompilerParams(
            dimension_semantics=("arbitrary",), vmem_limit_bytes=48 * 1024 * 1024
        ),
    )(*arrays)


def chain(matrices, addends, reverse):
    return pl.pallas_call(
        functools.partial(chain_kernel, reverse),
        out_shape=shape_of(addends),
        compiler_params=pltpu.CompilerParams(vmem_limit_bytes=48 * 1024 * 1024),
    )(matrices, addends)


def by_block(array):
    heads, rows = array.shape[:2]
    return jnp.swapaxes(array.reshape((heads, rows // SPAN, SPAN) + array.shape[2:]), 0, 1)


def by_head(array):
    blocks, heads, span = array.shape[:3]
    return jnp.swapaxes(array, 0, 1).reshape((heads, blocks * span) + array.shape[3:])


def exchange(parts):
    return lax.all_to_all(parts, "seq", 0, 0)


def columns_out(array, n):
    heads, rows, cols = array.shape
    parts = n // heads
    return (
        array.reshape(heads, rows, parts, cols // parts)
        .transpose(0, 2, 1, 3)
        .reshape(n, rows, cols // parts)
    )


def columns_in(array, heads):
    n, rows, width = array.shape
    parts = n // heads
    return (
        array.reshape(heads, parts, rows, width)
        .transpose(0, 2, 1, 3)
        .reshape(heads, rows, parts * width)
    )


def shards(
    block_in,
    first_norm_gain,
    w_query,
    w_key,
    w_value,
    w_gate,
    w_alpha,
    w_beta,
    conv_query,
    conv_key,
    conv_value,
    a_log,
    dt_bias,
    out_gain,
    w_out,
    second_norm_gain,
    w_ffgate,
    w_ffup,
    w_ffdown,
    cotangent,
):
    rows = block_in.shape[0]
    edge = CONV - 1
    n = lax.axis_size("seq")
    heads = a_log.shape[0]
    blocks = rows // SPAN
    width_k = w_query.shape[1]
    width_v = w_value.shape[1]
    width_f = w_ffgate.shape[1]
    width_m = 2 * width_k + width_v
    width_g = width_m + width_v

    def gather(*parts):
        return lax.all_gather(jnp.concatenate(parts, axis=1), "seq", axis=0, tiled=True)

    full_in = gather(w_query, w_key, w_value, w_gate, w_alpha, w_beta)
    full_o = gather(w_out.T)
    full_ff = gather(w_ffgate, w_ffup)
    full_fd = gather(w_ffdown.T)
    input_float = block_in.astype(jnp.float32)
    first_inverse_scale = rms_scale(input_float)
    first_unit_input = input_float * first_inverse_scale
    first_normed_input = (first_unit_input * first_norm_gain).astype(jnp.bfloat16)
    projected = matmul(first_normed_input, full_in)
    mix_pre = projected[:, :width_m].astype(jnp.bfloat16)
    gpre = projected[:, width_m:width_g].astype(jnp.bfloat16)
    a_lin = projected[:, width_g : width_g + heads]
    b_lin = projected[:, width_g + heads :]
    mix_taps = jnp.concatenate([conv_query, conv_key, conv_value], axis=1)
    before = from_behind(mix_pre[rows - edge :], "seq", 1)
    mix_ext = jnp.concatenate([before, mix_pre], axis=0).astype(jnp.float32)
    mixc = conv_apply(mix_ext, mix_taps, rows)
    prepared, prepare_back = jax.vjp(
        prepare,
        mixc[:, :width_k],
        mixc[:, width_k : 2 * width_k],
        mixc[:, 2 * width_k :],
        b_lin,
        a_lin,
        a_log,
        dt_bias,
    )
    query, keyvec, value = (by_block(a) for a in prepared[:3])
    beta, log_col = (by_block(a)[..., None] for a in prepared[3:])
    log_row = by_block(prepared[4])[:, :, None, :]
    items = (query, keyvec, value, beta, log_col, log_row)
    dim_k, dim_v = query.shape[-1], value.shape[-1]
    shape_k, shape_v = query.shape, value.shape
    shape_m = (blocks, heads, dim_k, dim_k)
    shape_s = (blocks, heads, dim_k, dim_v)
    empty, extent, matrix, addend, product, running = over_blocks(
        spans_kernel,
        blocks,
        0,
        (shape_v, shape_k, shape_m, shape_s, shape_m[1:], shape_s[1:]),
        2,
        (),
        False,
        *items,
    )
    parts = n // heads
    sent_matrices = jnp.broadcast_to(
        product[:, None], (heads, parts, dim_k, dim_k)
    ).reshape(n, dim_k, dim_k)
    matrices = exchange(sent_matrices)
    addends = exchange(columns_out(running, n))
    incoming = columns_in(exchange(chain(matrices, addends, False)), heads)
    block_result, states = over_blocks(
        apply_kernel,
        blocks,
        1,
        (shape_v, shape_s),
        0,
        (shape_s[1:],),
        False,
        empty,
        extent,
        matrix,
        addend,
        incoming,
    )
    on_f, finish_back = jax.vjp(finish, by_head(block_result), gpre.astype(jnp.float32), out_gain)
    on_b = on_f.astype(jnp.bfloat16)
    hidden_residual = input_float + pair_sum(matmul_tr(on_b, full_o))
    second_inverse_scale = rms_scale(hidden_residual)
    second_unit_input = hidden_residual * second_inverse_scale
    second_normed_input = (second_unit_input * second_norm_gain).astype(jnp.bfloat16)
    both = matmul(second_normed_input, full_ff)
    fg, fu = both[:, :width_f], both[:, width_f:]
    hid = (jax.nn.silu(fg) * fu).astype(jnp.bfloat16)
    fed = pair_sum(matmul_tr(hid, full_fd))
    block_out = (hidden_residual + fed).astype(jnp.bfloat16)
    feedforward_output_gradient = cotangent.astype(jnp.float32)
    dhid = matmul(cotangent, full_fd)
    sig = jax.nn.sigmoid(fg)
    dfu = (dhid * fg * sig).astype(jnp.bfloat16)
    dfg = (dhid * fu * sig * (1.0 + fg * (1.0 - sig))).astype(jnp.bfloat16)
    dboth = jnp.concatenate([dfg, dfu], axis=1)
    second_normed_gradient = pair_sum(matmul_tr(dboth, full_ff))
    second_norm_piece = jnp.sum(second_normed_gradient * second_unit_input, axis=0)
    hidden_gradient = feedforward_output_gradient + norm_gradient_step(
        second_normed_gradient * second_norm_gain, second_unit_input, second_inverse_scale
    )
    dh_b = hidden_gradient.astype(jnp.bfloat16)
    don = matmul(dh_b, full_o)
    output_gradient, dgpre, outgain_part = finish_back(don)
    outgain_part = pair_sum(outgain_part)
    output_gradient = by_block(output_gradient)
    (partial_gradient,) = over_blocks(
        partial_kernel, blocks, 0, (shape_s[1:],), 1, (), True, extent, matrix, output_gradient
    )
    behind = exchange(columns_out(partial_gradient, n))
    final_state_gradient = columns_in(exchange(chain(matrices, behind, True)), heads)

    def scatter(grad):
        return lax.psum_scatter(
            grad.astype(jnp.bfloat16), "seq", scatter_dimension=0, tiled=True
        ).astype(jnp.float32)

    dgb = dgpre.astype(jnp.bfloat16)
    sum_ffgate, sum_ffup = jnp.split(scatter(matmul_tl(second_normed_input, dboth)), 2, axis=1)
    sum_ffdown = scatter(matmul_tl(cotangent, hid)).T
    sum_out = scatter(matmul_tl(dh_b, on_b)).T
    sum_gate = scatter(matmul_tl(first_normed_input, dgb))
    grads = over_blocks(
        back_kernel,
        blocks,
        1,
        tuple(a.shape for a in items),
        0,
        (shape_s[1:],),
        True,
        *items,
        extent,
        matrix,
        states,
        output_gradient,
        final_state_gradient,
    )
    dq, dk, dv, dbeta, dlog_col, dlog_row = grads
    dlog = dlog_col[..., 0] + dlog_row[:, :, 0, :]
    grads_prepared = tuple(by_head(a) for a in (dq, dk, dv, dbeta[..., 0], dlog))
    dqc, dkc, dvc, db_lin, da_lin, alog_part, dt_part = prepare_back(grads_prepared)
    dmixc = jnp.concatenate([dqc, dkc, dvc], axis=1)
    after = from_behind(dmixc[:edge], "seq", -1)
    conv_part = conv_weight_grad(dmixc, mix_ext, rows)
    dmix = conv_back_apply(jnp.concatenate([dmixc, after], axis=0), mix_taps, rows)
    dcat = jnp.concatenate(
        [
            dmix.astype(jnp.bfloat16),
            dgb,
            da_lin.astype(jnp.bfloat16),
            db_lin.astype(jnp.bfloat16),
        ],
        axis=1,
    )
    dlate = jnp.concatenate([dcat[:, :width_m], dcat[:, width_g:]], axis=1)
    sum_late = scatter(matmul_tl(first_normed_input, dlate))
    sum_query = sum_late[:, :width_k]
    sum_key = sum_late[:, width_k : 2 * width_k]
    sum_value = sum_late[:, 2 * width_k : width_m]
    sum_alpha = sum_late[:, width_m : width_m + heads]
    sum_beta = sum_late[:, width_m + heads :]
    first_normed_gradient = pair_sum(matmul_tr(dcat, full_in))
    first_norm_piece = jnp.sum(first_normed_gradient * first_unit_input, axis=0)
    input_gradient = hidden_gradient + norm_gradient_step(
        first_normed_gradient * first_norm_gain, first_unit_input, first_inverse_scale
    )
    (
        grad_alog,
        grad_dt,
        grad_conv,
        first_norm_gain_gradient,
        second_norm_gain_gradient,
        grad_outgain,
    ) = lax.psum(
        (alog_part, dt_part, conv_part, first_norm_piece, second_norm_piece, outgain_part), "seq"
    )
    grad_convq = grad_conv[:, :width_k]
    grad_convk = grad_conv[:, width_k : 2 * width_k]
    grad_convv = grad_conv[:, 2 * width_k :]
    return (
        block_out,
        input_gradient,
        first_norm_gain_gradient,
        sum_query,
        sum_key,
        sum_value,
        sum_gate,
        sum_alpha,
        sum_beta,
        grad_convq,
        grad_convk,
        grad_convv,
        grad_alog,
        grad_dt,
        grad_outgain,
        sum_out,
        second_norm_gain_gradient,
        sum_ffgate,
        sum_ffup,
        sum_ffdown,
    )


def solution(mesh):
    placed = (
        P("seq", None),
        P(),
        P("seq", "head"),
        P("seq", "head"),
        P("seq", "head"),
        P("seq", "head"),
        P("seq", "head"),
        P("seq", "head"),
        P(None, "head"),
        P(None, "head"),
        P(None, "head"),
        P("head"),
        P("head"),
        P(),
        P("head", "seq"),
        P(),
        P("seq", "head"),
        P("seq", "head"),
        P("head", "seq"),
        P("seq", None),
    )
    return jax.shard_map(
        shards,
        mesh=mesh,
        in_specs=placed,
        out_specs=(
            P("seq", None),
            P("seq", None),
            P(),
            P("seq", "head"),
            P("seq", "head"),
            P("seq", "head"),
            P("seq", "head"),
            P("seq", "head"),
            P("seq", "head"),
            P(None, "head"),
            P(None, "head"),
            P(None, "head"),
            P("head"),
            P("head"),
            P(),
            P("head", "seq"),
            P(),
            P("seq", "head"),
            P("seq", "head"),
            P("head", "seq"),
        ),
        check_vma=False,
    )
```
